32 devices in a mesh: loop: 8 (over z, y), seg: 4 (over x, core).
Axes of the slice: x: 2, y: 2, z: 4, core: 2. Of those that a mesh axis runs over, the one named last changes fastest.
Arguments:
- dosage: bfloat16 [2048, 8192], P('seg', 'loop'), may hold values from -3 to 3
- weight_tiles: bfloat16 [3, 1024, 1024], P(None, None, 'loop'), may hold values from -0.109375 to 0.109375
- first_tile: int32 [1024], P('loop'), may hold values from 0 to 1
- last_tile: int32 [1024], P('loop'), may hold values from 1 to 2
Outputs:
- covariance: float32 [1024, 1024], P('seg', 'loop')
The draws below stay inside these ranges and needn't reach their ends.
Inputs may be any that keep to these rules, and one draw needn't show every extreme that they name: `first_tile`: a gene's window always covers its home slot 1.
All inputs are finite; a program needn't handle non-finite values.
Results may differ from the reference program's by a relative error of at most 0.0021.
Values may be sent and summed in bfloat16 or wider, within the bound.
No kernel may reach another device: no remote copies, remote signals or barrier semaphores. Data moves between devices by JAX's collectives and lax.ppermute only.
A program may use at most 64 MiB of HBM per device.

```python
import jax
import jax.numpy as jnp
from jax import lax

BLOCK = 1024
GENE_DEV = 128
REACH = 1
SPAN = 3
SAMPLES = 2048
VARIANTS = 8192
GENES = 1024


def touch_ends(array, own_key, smallest, top_value):
    shape = array.shape
    index_at = [jax.random.randint(jax.random.fold_in(own_key, axis), (), 0, shape[axis]) for axis in range(len(shape))]
    array = array.at[tuple(index_at)].set(smallest)
    longest = shape.index(max(shape))
    index_at[longest] = (index_at[longest] + 1) % shape[longest]
    return array.at[tuple(index_at)].set(top_value)


def block_scale(own_key, shape, cuts, least, largest):
    def one(axis_at, shards_of):
        steps = jax.random.uniform(jax.random.fold_in(jax.random.fold_in(own_key, 6), axis_at), (shards_of,), jnp.float32, least / len(cuts), largest / len(cuts))
        return jnp.repeat(jnp.exp(steps), shape[axis_at] // shards_of).reshape((-1,) + (1,) * (len(shape) - axis_at - 1))

    gain = one(*cuts[0])
    for cut in cuts[1:]:
        gain = gain * one(*cut)
    return gain


def gaussian(own_key, shape, width, most, cuts=(), held_as=jnp.bfloat16):
    gain = block_scale(own_key, shape, cuts, -0.22, 0.18) if cuts else 1.0
    values = jax.random.normal(own_key, shape, jnp.float32) * width * gain
    return jnp.minimum(jnp.maximum(values, -most), most).astype(held_as)


def setup_inputs(seed: int = 0) -> dict:
    streams_of = jax.random.split(jax.random.key(seed), 5)
    return {
        "dosage": gaussian(streams_of[0], (SAMPLES, VARIANTS), 0.6, 3.0, ((0, 4), (1, 8))),
        "weight_tiles": gaussian(streams_of[1], (SPAN, BLOCK, GENES), (SPAN * BLOCK) ** -0.5, 0.109375, ((2, 8),)),
        "first_tile": touch_ends(jax.random.randint(streams_of[2], (GENES,), 0, REACH + 1), jax.random.fold_in(streams_of[2], 1), 0, REACH).astype(jnp.int32),
        "last_tile": touch_ends(jax.random.randint(streams_of[3], (GENES,), REACH, SPAN), jax.random.fold_in(streams_of[3], 1), REACH, SPAN - 1).astype(jnp.int32),
    }


def reference(dosage, weight_tiles, first_tile, last_tile):
    blocks = VARIANTS // BLOCK
    slot_index = jnp.arange(SPAN, dtype=jnp.int32)[:, None]
    covered = (slot_index >= first_tile[None, :]) & (slot_index <= last_tile[None, :])
    masked = jnp.where(covered[:, None, :], weight_tiles, jnp.zeros((), weight_tiles.dtype))

    def one_block(home_block):
        running = jnp.zeros((SAMPLES, GENE_DEV), jnp.float32)
        for slot_pos in range(SPAN):
            source = home_block + slot_pos - REACH
            inside = (source >= 0) & (source < blocks)
            col_first = (jnp.clip(source, 0, blocks - 1) * BLOCK).astype(jnp.int32)
            columns = lax.dynamic_slice(dosage, (jnp.int32(0), col_first), (SAMPLES, BLOCK))
            gene_first = (home_block * GENE_DEV).astype(jnp.int32)
            moved_tile = lax.dynamic_slice(masked[slot_pos], (jnp.int32(0), gene_first), (BLOCK, GENE_DEV))
            pair_term = jnp.dot(columns, moved_tile, preferred_element_type=jnp.float32)
            running = running + jnp.where(inside, pair_term, jnp.zeros((), jnp.float32))
        return running.astype(jnp.bfloat16)

    pieces = lax.map(one_block, jnp.arange(blocks, dtype=jnp.int32))
    projection = jnp.transpose(pieces, (1, 0, 2)).reshape(SAMPLES, GENES)
    summed = lax.dot_general(projection, projection, (((0,), (0,)), ((), ())), preferred_element_type=jnp.float32)
    return summed / SAMPLES
```

```python
import functools

import jax
import jax.numpy as jnp
import numpy as np
from jax import lax
from jax.experimental import pallas as pl
from jax.experimental.pallas import tpu as pltpu
from jax.sharding import PartitionSpec as P

AXES = ("loop", "seg")


def ring_next(loop_size, place):
    if place % 2 == 0:
        return place + 2 if place + 2 < loop_size else loop_size - 1
    return place - 2 if place >= 3 else 0


def move(value, sizes, target):
    loop_size, seg_size = sizes
    pairs = []
    for place in range(loop_size):
        for part in range(seg_size):
            to = target(place, part)
            if to is not None and 0 <= to[0] < loop_size:
                pairs.append((place * seg_size + part, to[0] * seg_size + to[1]))
    return lax.ppermute(value, AXES, pairs)


def pair_kernel(n_blocks, per_chunk, where_ref, column_ref, *refs):
    blocks, (own_ref, away_ref) = refs[:n_blocks], refs[n_blocks:]
    genes = column_ref.shape[1]
    column = column_ref[...]
    for k, block in enumerate(blocks):
        product = lax.dot_general(block[...], column, (((0,), (0,)), ((), ())), preferred_element_type=jnp.float32)
        chunk = where_ref[2 * k]
        row = pl.multiple_of(where_ref[2 * k + 1] * genes, genes)

        @pl.when(chunk == 0)
        def _():
            own_ref[pl.ds(row, genes), :] = product

        @pl.when(chunk > 0)
        def _():
            away_ref[chunk - 1, pl.ds(row, genes), :] = product.astype(jnp.bfloat16)


def shards(dosage, weight_tiles, first_tile, last_tile):
    loop_size, seg_size = sizes = (lax.axis_size("loop"), lax.axis_size("seg"))
    place, part = lax.axis_index("loop"), lax.axis_index("seg")
    n_slots, block, genes = weight_tiles.shape
    samples = dosage.shape[0]
    odd, side = place % 2, part % 2
    half = block // 2

    def masked_half(slot):
        tile = lax.dynamic_slice(weight_tiles, (slot, side * half, 0), (1, half, genes))[0]
        covered = (slot >= first_tile) & (slot <= last_tile)
        return jnp.where(covered[None, :], tile, jnp.zeros((), tile.dtype))

    far_slot = odd * (n_slots - 1)
    far_half = masked_half(far_slot)
    near_half = masked_half(n_slots - 1 - far_slot)
    outward = lambda step: lambda l, s: (l + step if l % 2 else l - step, s)
    partner = lambda l, s: (l ^ 1, s)
    sibling = lambda l, s: (l, s ^ 1)

    far_half = move(far_half, sizes, outward(1))
    near_half = move(near_half, sizes, partner)

    def term(mine, other):
        lower = jnp.where(side == 0, mine, other)
        upper = jnp.where(side == 0, other, mine)
        return jnp.dot(dosage, jnp.concatenate([lower, upper], axis=0), preferred_element_type=jnp.float32)

    home_term = jnp.dot(dosage, weight_tiles[n_slots // 2], preferred_element_type=jnp.float32)
    home_term = move(home_term, sizes, partner)
    far_term = move(term(far_half, move(far_half, sizes, sibling)), sizes, outward(2))
    near_term = term(near_half, move(near_half, sizes, sibling))
    projection = (near_term + home_term + far_term).astype(jnp.bfloat16)

    column = move(projection, sizes, partner)
    ahead = [ring_next(loop_size, l) for l in range(loop_size)]
    behind = [ahead.index(l) for l in range(loop_size)]
    blocks, sources = [projection], [list(range(loop_size))]
    forth = back = projection
    forth_from = back_from = sources[0]
    for step in range(loop_size // 2):
        forth = move(forth, sizes, lambda l, s: (ahead[l], s))
        forth_from = [forth_from[behind[l]] for l in range(loop_size)]
        blocks.append(forth)
        sources.append(forth_from)
        if step + 1 < loop_size // 2:
            back = move(back, sizes, lambda l, s: (behind[l], s))
            back_from = [back_from[ahead[l]] for l in range(loop_size)]
            blocks.append(back)
            sources.append(back_from)

    per_chunk = loop_size // seg_size
    held = np.array(sources).T ^ 1
    parts = np.arange(seg_size)[None, :, None]
    table = np.stack([(held[:, None, :] // per_chunk) ^ parts, np.broadcast_to((held % per_chunk)[:, None, :], (loop_size, seg_size, loop_size))], axis=-1)
    table = jnp.asarray(table.reshape(loop_size * seg_size, -1), jnp.int32)
    where = lax.dynamic_slice(table, (place * seg_size + part, 0), (1, table.shape[1]))[0]
    rows = loop_size * genes // seg_size
    vmem = pl.BlockSpec(memory_space=pltpu.VMEM)
    own, away = pl.pallas_call(
        functools.partial(pair_kernel, loop_size, per_chunk),
        out_shape=(jax.ShapeDtypeStruct((rows, genes), jnp.float32), jax.ShapeDtypeStruct((seg_size - 1, rows, genes), jnp.bfloat16)),
        in_specs=[pl.BlockSpec(memory_space=pltpu.SMEM)] + [vmem] * (loop_size + 1),
        out_specs=(vmem, vmem),
        name="pair_sums",
    )(where, column, *blocks)
    total = own
    for j in range(1, seg_size):
        total = total + move(away[j - 1], sizes, lambda l, s: (l, s ^ j)).astype(jnp.float32)
    return total / (samples * seg_size)


def solution(mesh):
    return jax.shard_map(
        shards,
        mesh=mesh,
        in_specs=(P("seg", "loop"), P(None, None, "loop"), P("loop"), P("loop")),
        out_specs=P("seg", "loop"),
        check_vma=False,
    )
```

```python
import functools

import jax
import jax.numpy as jnp
import numpy as np
from jax import lax
from jax.experimental import pallas as pl
from jax.experimental.pallas import tpu as pltpu
from jax.sharding import PartitionSpec as P


AXES = ("loop", "seg")


def ring_next(loop_size, place):
    if place % 2 == 0:
        return place + 2 if place + 2 < loop_size else loop_size - 1
    return place - 2 if place >= 3 else 0


def move(value, sizes, target):
    loop_size, seg_size = sizes
    pairs = []
    for place in range(loop_size):
        for part in range(seg_size):
            to = target(place, part)
            if to is not None and 0 <= to[0] < loop_size:
                pairs.append((place * seg_size + part, to[0] * seg_size + to[1]))
    return lax.ppermute(value, AXES, pairs)


def pair_kernel(n_blocks, where_ref, column_ref, *refs):
    blocks, own_ref, away_refs, sums_ref = refs[:n_blocks], refs[n_blocks], refs[n_blocks + 1 : -1], refs[-1]
    genes = column_ref.shape[0]
    column = column_ref[...]
    for k, block in enumerate(blocks):
        product = lax.dot_general(block[...], column, (((1,), (1,)), ((), ())), preferred_element_type=jnp.float32)
        row = pl.multiple_of(where_ref[2 * k + 1] * genes, genes)
        sums_ref[where_ref[2 * k], pl.ds(row, genes), :] = product
    own_ref[...] = sums_ref[0]
    for j, away_ref in enumerate(away_refs):
        away_ref[...] = sums_ref[j + 1].astype(jnp.bfloat16)


def shards(dosage, weight_tiles, first_tile, last_tile):
    loop_size, seg_size = sizes = (lax.axis_size("loop"), lax.axis_size("seg"))
    place, part = lax.axis_index("loop"), lax.axis_index("seg")
    n_slots, block, genes = weight_tiles.shape
    samples = dosage.shape[0]
    odd, side = place % 2, part % 2
    half = block // 2

    def masked_half(slot):
        tile = lax.dynamic_slice(weight_tiles, (slot, side * half, 0), (1, half, genes))[0]
        covered = (slot >= first_tile) & (slot <= last_tile)
        return jnp.where(covered[None, :], tile, jnp.zeros((), tile.dtype))

    far_slot = odd * (n_slots - 1)
    far_half = masked_half(far_slot)
    near_half = masked_half(n_slots - 1 - far_slot)
    outward = lambda step: lambda l, s: (l + step if l % 2 else l - step, s)
    partner = lambda l, s: (l ^ 1, s)
    sibling = lambda l, s: (l, s ^ 1)

    def product(tile):
        return lax.dot_general(tile, dosage, (((0,), (1,)), ((), ())), preferred_element_type=jnp.float32)

    def term(mine, other):
        lower = jnp.where(side == 0, mine, other)
        upper = jnp.where(side == 0, other, mine)
        return product(jnp.concatenate([lower, upper], axis=0))

    far_half = move(far_half, sizes, outward(1))
    near_half = move(near_half, sizes, partner)
    home_term = product(weight_tiles[n_slots // 2])
    far_half, _ = lax.optimization_barrier((far_half, home_term))
    home_term = move(home_term, sizes, partner)
    far_term = term(far_half, move(far_half, sizes, sibling))
    near_half, _ = lax.optimization_barrier((near_half, far_term))
    far_term = move(far_term, sizes, outward(2))
    near_term = term(near_half, move(near_half, sizes, sibling))
    projection = (near_term + home_term + far_term).astype(jnp.bfloat16)

    column = move(projection, sizes, partner)
    ahead = [ring_next(loop_size, l) for l in range(loop_size)]
    behind = [ahead.index(l) for l in range(loop_size)]
    blocks, sources = [projection], [list(range(loop_size))]
    forth = back = projection
    forth_from = back_from = sources[0]
    for _ in range(loop_size // 2 - 1):
        forth = move(forth, sizes, lambda l, s: (ahead[l], s))
        forth_from = [forth_from[behind[l]] for l in range(loop_size)]
        back = move(back, sizes, lambda l, s: (behind[l], s))
        back_from = [back_from[ahead[l]] for l in range(loop_size)]
        blocks += [forth, back]
        sources += [forth_from, back_from]
    opposite = jnp.where(side == 0, forth, back)
    blocks.append(move(opposite, sizes, lambda l, s: (behind[l] if s % 2 else ahead[l], s)))
    sources.append([forth_from[behind[l]] for l in range(loop_size)])

    per_chunk = loop_size // seg_size
    held = np.array(sources).T ^ 1
    parts = np.arange(seg_size)[None, :, None]
    table = np.stack([(held[:, None, :] // per_chunk) ^ parts, np.broadcast_to((held % per_chunk)[:, None, :], (loop_size, seg_size, loop_size))], axis=-1)
    table = jnp.asarray(table.reshape(loop_size * seg_size, -1), jnp.int32)
    where = lax.dynamic_slice(table, (place * seg_size + part, 0), (1, table.shape[1]))[0]
    rows = loop_size * genes // seg_size
    vmem = pl.BlockSpec(memory_space=pltpu.VMEM)
    own, *away = pl.pallas_call(
        functools.partial(pair_kernel, loop_size),
        out_shape=[jax.ShapeDtypeStruct((rows, genes), jnp.float32)] + [jax.ShapeDtypeStruct((rows, genes), jnp.bfloat16)] * (seg_size - 1),
        in_specs=[pl.BlockSpec(memory_space=pltpu.SMEM)] + [vmem] * (loop_size + 1),
        out_specs=[vmem] * seg_size,
        scratch_shapes=[pltpu.VMEM((seg_size, rows, genes), jnp.float32)],
        compiler_params=pltpu.CompilerParams(vmem_limit_bytes=2 * (loop_size + 1) * genes * samples * 2 + 3 * seg_size * rows * genes * 4),
        name="pair_sums",
    )(where, column, *blocks)
    total = own
    for j in range(1, seg_size):
        total = total + move(away[j - 1], sizes, lambda l, s: (l, s ^ j)).astype(jnp.float32)
    return total / (samples * seg_size)


def solution(mesh):
    return jax.shard_map(
        shards,
        mesh=mesh,
        in_specs=(P("seg", "loop"), P(None, None, "loop"), P("loop"), P("loop")),
        out_specs=P("seg", "loop"),
        check_vma=False,
    )
```

```python
import functools

import jax
import jax.numpy as jnp
import numpy as np
from jax import lax
from jax.experimental import pallas as pl
from jax.experimental.pallas import tpu as pltpu
from jax.sharding import PartitionSpec as P


AXES = ("loop", "seg")


def ring_next(loop_size, place):
    if place % 2 == 0:
        return place + 2 if place + 2 < loop_size else loop_size - 1
    return place - 2 if place >= 3 else 0


def move(value, sizes, target):
    loop_size, seg_size = sizes
    pairs = []
    for place in range(loop_size):
        for part in range(seg_size):
            to = target(place, part)
            pairs.append((place * seg_size + part, to[0] * seg_size + to[1]))
    return lax.ppermute(value, AXES, pairs)


def pair_kernel(n_blocks, where_ref, column_ref, *refs):
    blocks, own_ref, away_refs, sums_ref = refs[:n_blocks], refs[n_blocks], refs[n_blocks + 1 : -1], refs[-1]
    genes = column_ref.shape[0]
    column = column_ref[...]
    for k, block in enumerate(blocks):
        product = lax.dot_general(block[...], column, (((1,), (1,)), ((), ())), preferred_element_type=jnp.float32)
        row = pl.multiple_of(where_ref[2 * k + 1] * genes, genes)
        sums_ref[where_ref[2 * k], pl.ds(row, genes), :] = product
    own_ref[...] = sums_ref[0]
    for j, away_ref in enumerate(away_refs):
        away_ref[...] = sums_ref[j + 1].astype(jnp.bfloat16)


def shards(dosage, weight_tiles, first_tile, last_tile):
    loop_size, seg_size = sizes = (lax.axis_size("loop"), lax.axis_size("seg"))
    place, part = lax.axis_index("loop"), lax.axis_index("seg")
    n_slots, block, genes = weight_tiles.shape
    samples = dosage.shape[0]
    odd, side = place % 2, part % 2
    half = block // 2

    def masked_half(slot, inside):
        tile = lax.dynamic_slice(weight_tiles, (slot, side * half, 0), (1, half, genes))[0]
        covered = (slot >= first_tile) & (slot <= last_tile) & inside
        return jnp.where(covered[None, :], tile, jnp.zeros((), tile.dtype))

    far_slot = odd * (n_slots - 1)
    far_half = masked_half(far_slot, (place > 0) & (place < loop_size - 1))
    near_half = masked_half(n_slots - 1 - far_slot, True)

    def outward(step):
        def target(l, s):
            to = l + step if l % 2 else l - step
            return (to if 0 <= to < loop_size else (l if step == 1 else (l - 2) % loop_size if l % 2 == 0 else (l + 2) % loop_size), s)

        return target

    partner = lambda l, s: (l ^ 1, s)
    sibling = lambda l, s: (l, s ^ 1)

    def product(tile):
        return lax.dot_general(tile, dosage, (((0,), (1,)), ((), ())), preferred_element_type=jnp.float32)

    def term(mine, other):
        lower = jnp.where(side == 0, mine, other)
        upper = jnp.where(side == 0, other, mine)
        return product(jnp.concatenate([lower, upper], axis=0))

    far_half = move(far_half, sizes, outward(1))
    near_half = move(near_half, sizes, partner)
    home_term = product(weight_tiles[n_slots // 2])
    far_half, _ = lax.optimization_barrier((far_half, home_term))
    home_term = move(home_term, sizes, partner)
    far_term = term(far_half, move(far_half, sizes, sibling))
    near_half, _ = lax.optimization_barrier((near_half, far_term))
    far_term = move(far_term.astype(jnp.bfloat16), sizes, outward(2))
    near_term = term(near_half, move(near_half, sizes, sibling))
    projection = (near_term + home_term + far_term).astype(jnp.bfloat16)

    ahead = [ring_next(loop_size, l) for l in range(loop_size)]
    behind = [ahead.index(l) for l in range(loop_size)]
    blocks, sources = [projection], [list(range(loop_size))]
    forth = back = projection
    forth_from = back_from = sources[0]
    for _ in range(loop_size // 2 - 1):
        forth = move(forth, sizes, lambda l, s: (ahead[l], s))
        forth_from = [forth_from[behind[l]] for l in range(loop_size)]
        back = move(back, sizes, lambda l, s: (behind[l], s))
        back_from = [back_from[ahead[l]] for l in range(loop_size)]
        blocks += [forth, back]
        sources += [forth_from, back_from]
    turns = [l for l in range(loop_size) if l ^ 1 in (ahead[l], behind[l])]
    column = move(projection, sizes, lambda l, s: (l if l in turns else l ^ 1, s))
    from_forth = functools.reduce(jnp.logical_or, [place == l for l in turns if behind[l] == l ^ 1])
    from_back = functools.reduce(jnp.logical_or, [place == l for l in turns if ahead[l] == l ^ 1])
    column = jnp.where(from_forth, blocks[1], jnp.where(from_back, blocks[2], column))
    opposite = jnp.where(side == 0, forth, back)
    blocks.append(move(opposite, sizes, lambda l, s: (behind[l] if s % 2 else ahead[l], s)))
    sources.append([forth_from[behind[l]] for l in range(loop_size)])

    per_chunk = loop_size // seg_size
    held = np.array(sources).T ^ 1
    parts = np.arange(seg_size)[None, :, None]
    table = np.stack([(held[:, None, :] // per_chunk) ^ parts, np.broadcast_to((held % per_chunk)[:, None, :], (loop_size, seg_size, loop_size))], axis=-1)
    table = jnp.asarray(table.reshape(loop_size * seg_size, -1), jnp.int32)
    where = lax.dynamic_slice(table, (place * seg_size + part, 0), (1, table.shape[1]))[0]
    rows = loop_size * genes // seg_size
    vmem = pl.BlockSpec(memory_space=pltpu.VMEM)
    own, *away = pl.pallas_call(
        functools.partial(pair_kernel, loop_size),
        out_shape=[jax.ShapeDtypeStruct((rows, genes), jnp.float32)] + [jax.ShapeDtypeStruct((rows, genes), jnp.bfloat16)] * (seg_size - 1),
        in_specs=[pl.BlockSpec(memory_space=pltpu.SMEM)] + [vmem] * (loop_size + 1),
        out_specs=[vmem] * seg_size,
        scratch_shapes=[pltpu.VMEM((seg_size, rows, genes), jnp.float32)],
        compiler_params=pltpu.CompilerParams(vmem_limit_bytes=2 * (loop_size + 1) * genes * samples * 2 + 3 * seg_size * rows * genes * 4),
        name="pair_sums",
    )(where, column, *blocks)
    total = own
    for j in range(1, seg_size):
        total = total + move(away[j - 1], sizes, lambda l, s: (l, s ^ j)).astype(jnp.float32)
    return total / (samples * seg_size)


def solution(mesh):
    return jax.shard_map(
        shards,
        mesh=mesh,
        in_specs=(P("seg", "loop"), P(None, None, "loop"), P("loop"), P("loop")),
        out_specs=P("seg", "loop"),
        check_vma=False,
    )
```

```python
import functools

import jax
import jax.numpy as jnp
import numpy as np
from jax import lax
from jax.experimental import pallas as pl
from jax.experimental.pallas import tpu as pltpu
from jax.sharding import PartitionSpec as P


AXES = ("loop", "seg")


def ring_next(loop_size, place):
    if place % 2 == 0:
        return place + 2 if place + 2 < loop_size else loop_size - 1
    return place - 2 if place >= 3 else 0


def move(value, sizes, target):
    loop_size, seg_size = sizes
    pairs = []
    for place in range(loop_size):
        for part in range(seg_size):
            to = target(place, part)
            pairs.append((place * seg_size + part, to[0] * seg_size + to[1]))
    return lax.ppermute(value, AXES, pairs)


def pair_kernel(n_blocks, where_ref, *refs):
    blocks, own_ref, away_refs = refs[:n_blocks], refs[n_blocks], refs[n_blocks + 1 : -2]
    column_ref, sums_ref = refs[-2:]
    genes = column_ref.shape[0]
    for k, block in enumerate(blocks):

        @pl.when(where_ref[2 * n_blocks] == k)
        def _():
            column_ref[...] = block[...]

    column = column_ref[...]
    for k, block in enumerate(blocks):
        product = lax.dot_general(block[...], column, (((1,), (1,)), ((), ())), preferred_element_type=jnp.float32)
        row = pl.multiple_of(where_ref[2 * k + 1] * genes, genes)
        sums_ref[where_ref[2 * k], pl.ds(row, genes), :] = product
    own_ref[...] = sums_ref[0]
    for j, away_ref in enumerate(away_refs):
        away_ref[...] = sums_ref[j + 1].astype(jnp.bfloat16)


def shards(dosage, weight_tiles, first_tile, last_tile):
    loop_size, seg_size = sizes = (lax.axis_size("loop"), lax.axis_size("seg"))
    place, part = lax.axis_index("loop"), lax.axis_index("seg")
    n_slots, block, genes = weight_tiles.shape
    samples = dosage.shape[0]
    odd, side = place % 2, part % 2
    half = block // 2

    def masked_half(slot, inside):
        tile = lax.dynamic_slice(weight_tiles, (slot, side * half, 0), (1, half, genes))[0]
        covered = (slot >= first_tile) & (slot <= last_tile) & inside
        return jnp.where(covered[None, :], tile, jnp.zeros((), tile.dtype))

    far_slot = odd * (n_slots - 1)
    far_half = masked_half(far_slot, (place > 0) & (place < loop_size - 1))
    near_half = masked_half(n_slots - 1 - far_slot, True)

    def outward(step):
        def target(l, s):
            to = l + step if l % 2 else l - step
            return (to if 0 <= to < loop_size else (l if step == 1 else (l - 2) % loop_size if l % 2 == 0 else (l + 2) % loop_size), s)

        return target

    partner = lambda l, s: (l ^ 1, s)
    sibling = lambda l, s: (l, s ^ 1)

    def product(tile):
        return lax.dot_general(tile, dosage, (((0,), (1,)), ((), ())), preferred_element_type=jnp.float32)

    def term(mine, other):
        lower = jnp.where(side == 0, mine, other)
        upper = jnp.where(side == 0, other, mine)
        return product(jnp.concatenate([lower, upper], axis=0))

    far_half = move(far_half, sizes, outward(1))
    near_half = move(near_half, sizes, partner)
    home_term = product(weight_tiles[n_slots // 2])
    far_half, _ = lax.optimization_barrier((far_half, home_term))
    home_term = move(home_term, sizes, partner)
    far_term = term(far_half, move(far_half, sizes, sibling))
    near_half, _ = lax.optimization_barrier((near_half, far_term))
    far_term = move(far_term.astype(jnp.bfloat16), sizes, outward(2))
    near_term = term(near_half, move(near_half, sizes, sibling))
    projection = (near_term + home_term + far_term).astype(jnp.bfloat16)

    ahead = [ring_next(loop_size, l) for l in range(loop_size)]
    behind = [ahead.index(l) for l in range(loop_size)]
    blocks, sources = [projection], [list(range(loop_size))]
    forth = back = projection
    forth_from = back_from = sources[0]
    for _ in range(loop_size // 2 - 1):
        forth = move(forth, sizes, lambda l, s: (ahead[l], s))
        forth_from = [forth_from[behind[l]] for l in range(loop_size)]
        back = move(back, sizes, lambda l, s: (behind[l], s))
        back_from = [back_from[ahead[l]] for l in range(loop_size)]
        blocks += [forth, back]
        sources += [forth_from, back_from]
    blocks.append(move(forth, sizes, lambda l, s: (ahead[l], s)))
    sources.append([forth_from[behind[l]] for l in range(loop_size)])

    per_chunk = loop_size // seg_size
    held = np.array(sources).T ^ 1
    parts = np.arange(seg_size)[None, :, None]
    table = np.stack([(held[:, None, :] // per_chunk) ^ parts, np.broadcast_to((held % per_chunk)[:, None, :], (loop_size, seg_size, loop_size))], axis=-1)
    table = table.reshape(loop_size * seg_size, 2 * loop_size)
    own_genes = np.argmax(held == np.arange(loop_size)[:, None], axis=1)
    table = jnp.asarray(np.concatenate([table, np.repeat(own_genes, seg_size)[:, None]], axis=1), jnp.int32)
    where = lax.dynamic_slice(table, (place * seg_size + part, 0), (1, table.shape[1]))[0]
    rows = loop_size * genes // seg_size
    vmem = pl.BlockSpec(memory_space=pltpu.VMEM)
    own, *away = pl.pallas_call(
        functools.partial(pair_kernel, loop_size),
        out_shape=[jax.ShapeDtypeStruct((rows, genes), jnp.float32)] + [jax.ShapeDtypeStruct((rows, genes), jnp.bfloat16)] * (seg_size - 1),
        in_specs=[pl.BlockSpec(memory_space=pltpu.SMEM)] + [vmem] * loop_size,
        out_specs=[vmem] * seg_size,
        scratch_shapes=[pltpu.VMEM((genes, samples), jnp.bfloat16), pltpu.VMEM((seg_size, rows, genes), jnp.float32)],
        compiler_params=pltpu.CompilerParams(vmem_limit_bytes=2 * (loop_size + 1) * genes * samples * 2 + 3 * seg_size * rows * genes * 4),
        name="pair_sums",
    )(where, *blocks)
    total = own
    for j in range(1, seg_size):
        total = total + move(away[j - 1], sizes, lambda l, s: (l, s ^ j)).astype(jnp.float32)
    return total / (samples * seg_size)


def solution(mesh):
    return jax.shard_map(
        shards,
        mesh=mesh,
        in_specs=(P("seg", "loop"), P(None, None, "loop"), P("loop"), P("loop")),
        out_specs=P("seg", "loop"),
        check_vma=False,
    )
```

```python
import functools

import jax
import jax.numpy as jnp
import numpy as np
from jax import lax
from jax.experimental import pallas as pl
from jax.experimental.pallas import tpu as pltpu
from jax.sharding import PartitionSpec as P


AXES = ("loop", "seg")


def ring_next(loop_size, place):
    if place % 2 == 0:
        return place + 2 if place + 2 < loop_size else loop_size - 1
    return place - 2 if place >= 3 else 0


def move(value, sizes, target):
    loop_size, seg_size = sizes
    pairs = []
    for place in range(loop_size):
        for part in range(seg_size):
            to = target(place, part)
            pairs.append((place * seg_size + part, to[0] * seg_size + to[1]))
    return lax.ppermute(value, AXES, pairs)


def pair_kernel(n_blocks, where_ref, *refs):
    blocks, own_ref, away_refs = refs[:n_blocks], refs[n_blocks], refs[n_blocks + 1 : -2]
    column_ref, sums_ref = refs[-2:]
    genes = column_ref.shape[0]
    for k, block in enumerate(blocks):

        @pl.when(where_ref[2 * n_blocks] == k)
        def _():
            column_ref[...] = block[...]

    column = column_ref[...]
    for k, block in enumerate(blocks):
        product = lax.dot_general(block[...], column, (((1,), (1,)), ((), ())), preferred_element_type=jnp.float32)
        row = pl.multiple_of(where_ref[2 * k + 1] * genes, genes)
        sums_ref[where_ref[2 * k], pl.ds(row, genes), :] = product
    own_ref[...] = sums_ref[0]
    for j, away_ref in enumerate(away_refs):
        away_ref[...] = sums_ref[j + 1].astype(jnp.bfloat16)


def shards(dosage, weight_tiles, first_tile, last_tile):
    loop_size, seg_size = sizes = (lax.axis_size("loop"), lax.axis_size("seg"))
    place, part = lax.axis_index("loop"), lax.axis_index("seg")
    n_slots, block, genes = weight_tiles.shape
    samples = dosage.shape[0]
    odd, side = place % 2, part % 2
    half = block // 2

    def masked_half(slot, inside):
        tile = lax.dynamic_slice(weight_tiles, (slot, side * half, 0), (1, half, genes))[0]
        covered = (slot >= first_tile) & (slot <= last_tile) & inside
        return jnp.where(covered[None, :], tile, jnp.zeros((), tile.dtype))

    far_slot = odd * (n_slots - 1)
    far_half = masked_half(far_slot, (place > 0) & (place < loop_size - 1))
    near_half = masked_half(n_slots - 1 - far_slot, True)

    def outward(step):
        def target(l, s):
            to = l + step if l % 2 else l - step
            return (to if 0 <= to < loop_size else (l if step == 1 else (l - 2) % loop_size if l % 2 == 0 else (l + 2) % loop_size), s)

        return target

    partner = lambda l, s: (l ^ 1, s)
    sibling = lambda l, s: (l, s ^ 1)

    def product(tile):
        return lax.dot_general(tile, dosage, (((0,), (1,)), ((), ())), preferred_element_type=jnp.float32)

    def term(mine, other):
        lower = jnp.where(side == 0, mine, other)
        upper = jnp.where(side == 0, other, mine)
        return product(jnp.concatenate([lower, upper], axis=0))

    far_half = move(far_half, sizes, outward(1))
    near_half = move(near_half, sizes, partner)
    home_term = product(weight_tiles[n_slots // 2])
    far_half, _ = lax.optimization_barrier((far_half, home_term))
    home_term = move(home_term, sizes, partner)
    far_term = term(far_half, move(far_half, sizes, sibling))
    near_half, _ = lax.optimization_barrier((near_half, far_term))
    far_term = move(far_term.astype(jnp.bfloat16), sizes, outward(2))
    near_term = term(near_half, move(near_half, sizes, sibling))
    projection = (near_term + home_term + far_term).astype(jnp.bfloat16)

    ahead = [ring_next(loop_size, l) for l in range(loop_size)]
    behind = [ahead.index(l) for l in range(loop_size)]
    blocks, sources = [projection], [list(range(loop_size))]
    forth = back = projection
    forth_from = back_from = sources[0]
    rounds = loop_size // 2 - 1
    for step in range(rounds):
        if step == rounds - 1:
            opposite = jnp.where(side == 0, forth, back)
            opposite = move(opposite, sizes, lambda l, s: (behind[behind[l]] if s % 2 else ahead[ahead[l]], s))
            opposite_from = [forth_from[behind[behind[l]]] for l in range(loop_size)]
        forth = move(forth, sizes, lambda l, s: (ahead[l], s))
        forth_from = [forth_from[behind[l]] for l in range(loop_size)]
        back = move(back, sizes, lambda l, s: (behind[l], s))
        back_from = [back_from[ahead[l]] for l in range(loop_size)]
        blocks += [forth, back]
        sources += [forth_from, back_from]
    blocks.append(opposite)
    sources.append(opposite_from)

    per_chunk = loop_size // seg_size
    held = np.array(sources).T ^ 1
    parts = np.arange(seg_size)[None, :, None]
    table = np.stack([(held[:, None, :] // per_chunk) ^ parts, np.broadcast_to((held % per_chunk)[:, None, :], (loop_size, seg_size, loop_size))], axis=-1)
    table = table.reshape(loop_size * seg_size, 2 * loop_size)
    own_genes = np.argmax(held == np.arange(loop_size)[:, None], axis=1)
    table = jnp.asarray(np.concatenate([table, np.repeat(own_genes, seg_size)[:, None]], axis=1), jnp.int32)
    where = lax.dynamic_slice(table, (place * seg_size + part, 0), (1, table.shape[1]))[0]
    rows = loop_size * genes // seg_size
    vmem = pl.BlockSpec(memory_space=pltpu.VMEM)
    own, *away = pl.pallas_call(
        functools.partial(pair_kernel, loop_size),
        out_shape=[jax.ShapeDtypeStruct((rows, genes), jnp.float32)] + [jax.ShapeDtypeStruct((rows, genes), jnp.bfloat16)] * (seg_size - 1),
        in_specs=[pl.BlockSpec(memory_space=pltpu.SMEM)] + [vmem] * loop_size,
        out_specs=[vmem] * seg_size,
        scratch_shapes=[pltpu.VMEM((genes, samples), jnp.bfloat16), pltpu.VMEM((seg_size, rows, genes), jnp.float32)],
        compiler_params=pltpu.CompilerParams(vmem_limit_bytes=2 * (loop_size + 1) * genes * samples * 2 + 3 * seg_size * rows * genes * 4),
        name="pair_sums",
    )(where, *blocks)
    total = own
    for j in range(1, seg_size):
        total = total + move(away[j - 1], sizes, lambda l, s: (l, s ^ j)).astype(jnp.float32)
    return total / (samples * seg_size)


def solution(mesh):
    return jax.shard_map(
        shards,
        mesh=mesh,
        in_specs=(P("seg", "loop"), P(None, None, "loop"), P("loop"), P("loop")),
        out_specs=P("seg", "loop"),
        check_vma=False,
    )
```

```python
import functools

import jax
import jax.numpy as jnp
import numpy as np
from jax import lax
from jax.experimental import pallas as pl
from jax.experimental.pallas import tpu as pltpu
from jax.sharding import PartitionSpec as P


AXES = ("loop", "seg")


def ring_next(loop_size, place):
    if place % 2 == 0:
        return place + 2 if place + 2 < loop_size else loop_size - 1
    return place - 2 if place >= 3 else 0


def move(value, sizes, target):
    loop_size, seg_size = sizes
    pairs = []
    for place in range(loop_size):
        for part in range(seg_size):
            to = target(place, part)
            pairs.append((place * seg_size + part, to[0] * seg_size + to[1]))
    return lax.ppermute(value, AXES, pairs)


def pair_kernel(n_blocks, where_ref, *refs):
    blocks, own_ref, away_refs = refs[:n_blocks], refs[n_blocks], refs[n_blocks + 1 : -2]
    column_ref, sums_ref = refs[-2:]
    genes = column_ref.shape[0]
    for k, block in enumerate(blocks):

        @pl.when(where_ref[2 * n_blocks] == k)
        def _():
            column_ref[...] = block[...]

    column = column_ref[...].T
    for k, block in enumerate(blocks):
        product = jnp.dot(block[...], column, preferred_element_type=jnp.float32)
        row = pl.multiple_of(where_ref[2 * k + 1] * genes, genes)
        sums_ref[where_ref[2 * k], pl.ds(row, genes), :] = product
    own_ref[...] = sums_ref[0]
    for j, away_ref in enumerate(away_refs):
        away_ref[...] = sums_ref[j + 1].astype(jnp.bfloat16)


def shards(dosage, weight_tiles, first_tile, last_tile):
    loop_size, seg_size = sizes = (lax.axis_size("loop"), lax.axis_size("seg"))
    place, part = lax.axis_index("loop"), lax.axis_index("seg")
    n_slots, block, genes = weight_tiles.shape
    samples = dosage.shape[0]
    odd, side = place % 2, part % 2
    half = block // 2

    far_slot = odd * (n_slots - 1)
    near_slot = n_slots - 1 - far_slot

    def half_tile(slot):
        return lax.dynamic_slice(weight_tiles, (slot, side * half, 0), (1, half, genes))[0]

    def covered(slot):
        return ((slot >= first_tile) & (slot <= last_tile))[None, :]

    far_half = half_tile(far_slot)
    far_mask = covered(far_slot) & (place > 0) & (place < loop_size - 1)
    near_half = jnp.where(covered(near_slot), half_tile(near_slot), jnp.zeros((), weight_tiles.dtype))
    near_half = jnp.concatenate([near_half, jnp.broadcast_to(far_mask, (16, genes)).astype(near_half.dtype)], axis=0)

    def outward(step):
        def target(l, s):
            to = l + step if l % 2 else l - step
            return (to if 0 <= to < loop_size else (l if step == 1 else (l - 2) % loop_size if l % 2 == 0 else (l + 2) % loop_size), s)

        return target

    partner = lambda l, s: (l ^ 1, s)
    sibling = lambda l, s: (l, s ^ 1)

    def product(tile):
        return lax.dot_general(tile, dosage, (((0,), (1,)), ((), ())), preferred_element_type=jnp.float32)

    def term(mine, other):
        lower = jnp.where(side == 0, mine, other)
        upper = jnp.where(side == 0, other, mine)
        return product(jnp.concatenate([lower, upper], axis=0))

    far_half = move(far_half, sizes, outward(1))
    near_half = move(near_half, sizes, partner)
    home_term = product(weight_tiles[n_slots // 2])
    far_half, _ = lax.optimization_barrier((far_half, home_term))
    home_term = move(home_term, sizes, partner)
    far_term = term(far_half, move(far_half, sizes, sibling))
    near_half, _ = lax.optimization_barrier((near_half, far_term))
    near_half, far_mask = near_half[:half], near_half[half]
    far_term = move(far_term.astype(jnp.bfloat16), sizes, outward(2))
    near_term = term(near_half, move(near_half, sizes, sibling))
    far_term = jnp.where(far_mask[:, None] > 0, far_term.astype(jnp.float32), 0.0)
    projection = (near_term + home_term + far_term).astype(jnp.bfloat16)

    ahead = [ring_next(loop_size, l) for l in range(loop_size)]
    behind = [ahead.index(l) for l in range(loop_size)]
    blocks, sources = [projection], [list(range(loop_size))]
    forth = back = projection
    forth_from = back_from = sources[0]
    rounds = loop_size // 2 - 1
    for step in range(rounds):
        if step == rounds - 1:
            opposite = jnp.where(side == 0, forth, back)
            opposite = move(opposite, sizes, lambda l, s: (behind[behind[l]] if s % 2 else ahead[ahead[l]], s))
            opposite_from = [forth_from[behind[behind[l]]] for l in range(loop_size)]
        forth = move(forth, sizes, lambda l, s: (ahead[l], s))
        forth_from = [forth_from[behind[l]] for l in range(loop_size)]
        back = move(back, sizes, lambda l, s: (behind[l], s))
        back_from = [back_from[ahead[l]] for l in range(loop_size)]
        blocks += [forth, back]
        sources += [forth_from, back_from]
    blocks.append(opposite)
    sources.append(opposite_from)

    per_chunk = loop_size // seg_size
    held = np.array(sources).T ^ 1
    parts = np.arange(seg_size)[None, :, None]
    table = np.stack([(held[:, None, :] // per_chunk) ^ parts, np.broadcast_to((held % per_chunk)[:, None, :], (loop_size, seg_size, loop_size))], axis=-1)
    table = table.reshape(loop_size * seg_size, 2 * loop_size)
    own_genes = np.argmax(held == np.arange(loop_size)[:, None], axis=1)
    table = jnp.asarray(np.concatenate([table, np.repeat(own_genes, seg_size)[:, None]], axis=1), jnp.int32)
    where = lax.dynamic_slice(table, (place * seg_size + part, 0), (1, table.shape[1]))[0]
    rows = loop_size * genes // seg_size
    vmem = pl.BlockSpec(memory_space=pltpu.VMEM)
    own, *away = pl.pallas_call(
        functools.partial(pair_kernel, loop_size),
        out_shape=[jax.ShapeDtypeStruct((rows, genes), jnp.float32)] + [jax.ShapeDtypeStruct((rows, genes), jnp.bfloat16)] * (seg_size - 1),
        in_specs=[pl.BlockSpec(memory_space=pltpu.SMEM)] + [vmem] * loop_size,
        out_specs=[vmem] * seg_size,
        scratch_shapes=[pltpu.VMEM((genes, samples), jnp.bfloat16), pltpu.VMEM((seg_size, rows, genes), jnp.float32)],
        compiler_params=pltpu.CompilerParams(vmem_limit_bytes=2 * (loop_size + 1) * genes * samples * 2 + 3 * seg_size * rows * genes * 4),
        name="pair_sums",
    )(where, *blocks)
    total = own
    for j in range(1, seg_size):
        total = total + move(away[j - 1], sizes, lambda l, s: (l, s ^ j)).astype(jnp.float32)
    return total / (samples * seg_size)


def solution(mesh):
    return jax.shard_map(
        shards,
        mesh=mesh,
        in_specs=(P("seg", "loop"), P(None, None, "loop"), P("loop"), P("loop")),
        out_specs=P("seg", "loop"),
        check_vma=False,
    )
```

```python
import functools
import math

import jax
import jax.numpy as jnp
import numpy as np
from jax import lax
from jax.experimental import pallas as pl
from jax.experimental.pallas import tpu as pltpu
from jax.sharding import PartitionSpec as P


AXES = ("loop", "seg")
DOSAGE_MAX, WEIGHT_MAX = 3.0, 0.109375


def ring_next(loop_size, place):
    if place % 2 == 0:
        return place + 2 if place + 2 < loop_size else loop_size - 1
    return place - 2 if place >= 3 else 0


def move(value, sizes, target):
    loop_size, seg_size = sizes
    pairs = []
    for place in range(loop_size):
        for part in range(seg_size):
            to = target(place, part)
            pairs.append((place * seg_size + part, to[0] * seg_size + to[1]))
    return lax.ppermute(value, AXES, pairs)


def pair_kernel(n_blocks, where_ref, *refs):
    blocks, own_ref, away_refs = refs[:n_blocks], refs[n_blocks], refs[n_blocks + 1 : -2]
    column_ref, sums_ref = refs[-2:]
    genes = column_ref.shape[0]
    for k, block in enumerate(blocks):

        @pl.when(where_ref[2 * n_blocks] == k)
        def _():
            column_ref[...] = block[...]

    column = column_ref[...].T
    for k, block in enumerate(blocks):
        product = jnp.dot(block[...], column, preferred_element_type=jnp.float32)
        row = pl.multiple_of(where_ref[2 * k + 1] * genes, genes)
        sums_ref[where_ref[2 * k], pl.ds(row, genes), :] = product
    own_ref[...] = sums_ref[0]
    for j, away_ref in enumerate(away_refs):
        away_ref[...] = sums_ref[j + 1].astype(jnp.bfloat16)


def shards(dosage, weight_tiles, first_tile, last_tile):
    loop_size, seg_size = sizes = (lax.axis_size("loop"), lax.axis_size("seg"))
    place, part = lax.axis_index("loop"), lax.axis_index("seg")
    n_slots, block, genes = weight_tiles.shape
    samples = dosage.shape[0]
    odd, side = place % 2, part % 2
    half = block // 2

    far_slot = odd * (n_slots - 1)
    near_slot = n_slots - 1 - far_slot

    def half_tile(slot):
        return lax.dynamic_slice(weight_tiles, (slot, side * half, 0), (1, half, genes))[0]

    def covered(slot):
        return ((slot >= first_tile) & (slot <= last_tile))[None, :]

    far_half = half_tile(far_slot)
    far_mask = covered(far_slot) & (place > 0) & (place < loop_size - 1)
    near_half = jnp.where(covered(near_slot), half_tile(near_slot), jnp.zeros((), weight_tiles.dtype))
    near_half = jnp.concatenate([near_half, jnp.broadcast_to(far_mask, (16, genes)).astype(near_half.dtype)], axis=0)

    def outward(step):
        def target(l, s):
            to = l + step if l % 2 else l - step
            return (to if 0 <= to < loop_size else (l if step == 1 else l ^ 1), s)

        return target

    partner = lambda l, s: (l ^ 1, s)
    sibling = lambda l, s: (l, s ^ 1)

    scale = 2.0 ** math.floor(math.log2(float(jnp.finfo(jnp.float16).max) / (block * DOSAGE_MAX * WEIGHT_MAX)))

    def packed(term):
        return (term * scale).astype(jnp.float16)

    def product(tile):
        return lax.dot_general(tile, dosage, (((0,), (1,)), ((), ())), preferred_element_type=jnp.float32)

    def term(mine, other):
        lower = jnp.where(side == 0, mine, other)
        upper = jnp.where(side == 0, other, mine)
        return product(jnp.concatenate([lower, upper], axis=0))

    far_half = move(far_half, sizes, outward(1))
    near_half = move(near_half, sizes, partner)
    home_term = product(weight_tiles[n_slots // 2])
    far_half, _ = lax.optimization_barrier((far_half, home_term))
    home_term = move(packed(home_term), sizes, partner)
    far_term = term(far_half, move(far_half, sizes, sibling))
    near_half, _ = lax.optimization_barrier((near_half, far_term))
    near_half, far_mask = near_half[:half], near_half[half]
    far_term = move(packed(far_term), sizes, outward(2))
    near_term = term(near_half, move(near_half, sizes, sibling))
    far_term = jnp.where(far_mask[:, None] > 0, far_term.astype(jnp.float32), 0.0)
    projection = (near_term + (home_term.astype(jnp.float32) + far_term) * (1.0 / scale)).astype(jnp.bfloat16)

    ahead = [ring_next(loop_size, l) for l in range(loop_size)]
    behind = [ahead.index(l) for l in range(loop_size)]
    blocks, sources = [projection], [list(range(loop_size))]
    forth = back = projection
    forth_from = back_from = sources[0]
    rounds = loop_size // 2 - 1
    for step in range(rounds):
        if step == rounds - 1:
            opposite = jnp.where(side == 0, forth, back)
            opposite = move(opposite, sizes, lambda l, s: (behind[behind[l]] if s % 2 else ahead[ahead[l]], s))
            opposite_from = [forth_from[behind[behind[l]]] for l in range(loop_size)]
        forth = move(forth, sizes, lambda l, s: (ahead[l], s))
        forth_from = [forth_from[behind[l]] for l in range(loop_size)]
        back = move(back, sizes, lambda l, s: (behind[l], s))
        back_from = [back_from[ahead[l]] for l in range(loop_size)]
        blocks += [forth, back]
        sources += [forth_from, back_from]
    blocks.append(opposite)
    sources.append(opposite_from)

    per_chunk = loop_size // seg_size
    held = np.array(sources).T ^ 1
    parts = np.arange(seg_size)[None, :, None]
    table = np.stack([(held[:, None, :] // per_chunk) ^ parts, np.broadcast_to((held % per_chunk)[:, None, :], (loop_size, seg_size, loop_size))], axis=-1)
    table = table.reshape(loop_size * seg_size, 2 * loop_size)
    own_genes = np.argmax(held == np.arange(loop_size)[:, None], axis=1)
    table = jnp.asarray(np.concatenate([table, np.repeat(own_genes, seg_size)[:, None]], axis=1), jnp.int32)
    where = lax.dynamic_slice(table, (place * seg_size + part, 0), (1, table.shape[1]))[0]
    rows = loop_size * genes // seg_size
    vmem = pl.BlockSpec(memory_space=pltpu.VMEM)
    own, *away = pl.pallas_call(
        functools.partial(pair_kernel, loop_size),
        out_shape=[jax.ShapeDtypeStruct((rows, genes), jnp.float32)] + [jax.ShapeDtypeStruct((rows, genes), jnp.bfloat16)] * (seg_size - 1),
        in_specs=[pl.BlockSpec(memory_space=pltpu.SMEM)] + [vmem] * loop_size,
        out_specs=[vmem] * seg_size,
        scratch_shapes=[pltpu.VMEM((genes, samples), jnp.bfloat16), pltpu.VMEM((seg_size, rows, genes), jnp.float32)],
        compiler_params=pltpu.CompilerParams(vmem_limit_bytes=2 * (loop_size + 1) * genes * samples * 2 + 3 * seg_size * rows * genes * 4),
        name="pair_sums",
    )(where, *blocks)
    total = own
    for j in range(1, seg_size):
        total = total + move(away[j - 1], sizes, lambda l, s: (l, s ^ j)).astype(jnp.float32)
    return total / (samples * seg_size)


def solution(mesh):
    return jax.shard_map(
        shards,
        mesh=mesh,
        in_specs=(P("seg", "loop"), P(None, None, "loop"), P("loop"), P("loop")),
        out_specs=P("seg", "loop"),
        check_vma=False,
    )
```

```python
import functools
import math

import jax
import jax.numpy as jnp
import numpy as np
from jax import lax
from jax.experimental import pallas as pl
from jax.experimental.pallas import tpu as pltpu
from jax.sharding import PartitionSpec as P


AXES = ("loop", "seg")
DOSAGE_MAX, WEIGHT_MAX = 3.0, 0.109375
MASK_ROWS = 16


def ring_next(loop_size, place):
    if place % 2 == 0:
        return place + 2 if place + 2 < loop_size else loop_size - 1
    return place - 2 if place >= 3 else 0


def move(value, sizes, target):
    loop_size, seg_size = sizes
    pairs = []
    for place in range(loop_size):
        for part in range(seg_size):
            to = target(place, part)
            pairs.append((place * seg_size + part, to[0] * seg_size + to[1]))
    return lax.ppermute(value, AXES, pairs)


def stage_kernel(weights_ref, first_ref, last_ref, far_ref, near_ref, home_ref, tile_ref, window_ref, sems):
    place, part = lax.axis_index("loop"), lax.axis_index("seg")
    n_slots = weights_ref.shape[0]
    half = far_ref.shape[0]
    far_slot = (place % 2) * (n_slots - 1)
    near_slot = n_slots - 1 - far_slot
    rows = pl.ds(pl.multiple_of((part % 2) * half, half), half)
    copies = [
        pltpu.make_async_copy(weights_ref.at[far_slot, rows], far_ref, sems.at[0]),
        pltpu.make_async_copy(first_ref, window_ref.at[0], sems.at[1]),
        pltpu.make_async_copy(last_ref, window_ref.at[1], sems.at[2]),
        pltpu.make_async_copy(weights_ref.at[near_slot, rows], tile_ref, sems.at[3]),
        pltpu.make_async_copy(weights_ref.at[n_slots // 2], home_ref, sems.at[4]),
    ]
    for copy in copies:
        copy.start()
    for copy in copies[1:4]:
        copy.wait()
    first, last = window_ref[0], window_ref[1]
    covered = (near_slot >= first) & (near_slot <= last)
    near_ref[:half, :] = jnp.where(covered, tile_ref[...], jnp.zeros((), tile_ref.dtype))
    covered = (far_slot >= first) & (far_slot <= last) & (place > 0) & (place < lax.axis_size("loop") - 1)
    mask = jnp.where(covered, 1.0, 0.0)
    near_ref[half:, :] = jnp.broadcast_to(mask, (MASK_ROWS, mask.shape[1])).astype(near_ref.dtype)
    copies[0].wait()
    copies[4].wait()


def pair_kernel(n_blocks, where_ref, *refs):
    blocks, own_ref, away_refs = refs[:n_blocks], refs[n_blocks], refs[n_blocks + 1 : -2]
    column_ref, sums_ref = refs[-2:]
    genes = column_ref.shape[0]
    for k, block in enumerate(blocks):

        @pl.when(where_ref[2 * n_blocks] == k)
        def _():
            column_ref[...] = block[...]

    column = column_ref[...].T
    for k, block in enumerate(blocks):
        product = jnp.dot(block[...], column, preferred_element_type=jnp.float32)
        row = pl.multiple_of(where_ref[2 * k + 1] * genes, genes)
        sums_ref[where_ref[2 * k], pl.ds(row, genes), :] = product
    own_ref[...] = sums_ref[0]
    for j, away_ref in enumerate(away_refs):
        away_ref[...] = sums_ref[j + 1].astype(jnp.bfloat16)


def shards(dosage, weight_tiles, first_tile, last_tile):
    loop_size, seg_size = sizes = (lax.axis_size("loop"), lax.axis_size("seg"))
    place, part = lax.axis_index("loop"), lax.axis_index("seg")
    _, block, genes = weight_tiles.shape
    samples = dosage.shape[0]
    side = part % 2
    half = block // 2

    vmem = pl.BlockSpec(memory_space=pltpu.VMEM)
    hbm = pl.BlockSpec(memory_space=pltpu.HBM)
    tile_of = lambda n: jax.ShapeDtypeStruct((n, genes), weight_tiles.dtype)
    far_half, near_half, home_tile = pl.pallas_call(
        stage_kernel,
        out_shape=(tile_of(half), tile_of(half + MASK_ROWS), tile_of(block)),
        in_specs=[hbm] * 3,
        out_specs=[vmem] * 3,
        scratch_shapes=[pltpu.VMEM((half, genes), weight_tiles.dtype), pltpu.VMEM((2, 1, genes), jnp.int32), pltpu.SemaphoreType.DMA((5,))],
        compiler_params=pltpu.CompilerParams(vmem_limit_bytes=8 * block * genes * 2),
        name="stage",
    )(*[pltpu.with_memory_space_constraint(x, pltpu.HBM) for x in (weight_tiles, first_tile.reshape(1, -1), last_tile.reshape(1, -1))])

    def outward(step):
        def target(l, s):
            to = l + step if l % 2 else l - step
            return (to if 0 <= to < loop_size else (l if step == 1 else l ^ 1), s)

        return target

    partner = lambda l, s: (l ^ 1, s)
    sibling = lambda l, s: (l, s ^ 1)

    scale = 2.0 ** math.floor(math.log2(float(jnp.finfo(jnp.float16).max) / (block * DOSAGE_MAX * WEIGHT_MAX)))

    def packed(term):
        return (term * scale).astype(jnp.float16)

    def product(tile):
        return lax.dot_general(tile, dosage, (((0,), (1,)), ((), ())), preferred_element_type=jnp.float32)

    def term(mine, other):
        lower = jnp.where(side == 0, mine, other)
        upper = jnp.where(side == 0, other, mine)
        return product(jnp.concatenate([lower, upper], axis=0))

    far_half = move(far_half, sizes, outward(1))
    near_half = move(near_half, sizes, partner)
    home_term = product(home_tile)
    far_half, _ = lax.optimization_barrier((far_half, home_term))
    home_term = move(packed(home_term), sizes, partner)
    far_term = term(far_half, move(far_half, sizes, sibling))
    near_half, _ = lax.optimization_barrier((near_half, far_term))
    near_half, far_mask = near_half[:half], near_half[half]
    far_term = move(packed(far_term), sizes, outward(2))
    near_term = term(near_half, move(near_half, sizes, sibling))
    far_term = jnp.where(far_mask[:, None] > 0, far_term.astype(jnp.float32), 0.0)
    ready = lax.optimization_barrier(near_term + home_term.astype(jnp.float32) * (1.0 / scale))
    projection = (ready + far_term * (1.0 / scale)).astype(jnp.bfloat16)

    ahead = [ring_next(loop_size, l) for l in range(loop_size)]
    behind = [ahead.index(l) for l in range(loop_size)]
    blocks, sources = [projection], [list(range(loop_size))]
    forth = back = projection
    forth_from = back_from = sources[0]
    rounds = loop_size // 2 - 1
    for step in range(rounds):
        if step == rounds - 1:
            opposite = jnp.where(side == 0, forth, back)
            opposite = move(opposite, sizes, lambda l, s: (behind[behind[l]] if s % 2 else ahead[ahead[l]], s))
            opposite_from = [forth_from[behind[behind[l]]] for l in range(loop_size)]
        forth = move(forth, sizes, lambda l, s: (ahead[l], s))
        forth_from = [forth_from[behind[l]] for l in range(loop_size)]
        back = move(back, sizes, lambda l, s: (behind[l], s))
        back_from = [back_from[ahead[l]] for l in range(loop_size)]
        blocks += [forth, back]
        sources += [forth_from, back_from]
    blocks.append(opposite)
    sources.append(opposite_from)

    per_chunk = loop_size // seg_size
    held = np.array(sources).T ^ 1
    parts = np.arange(seg_size)[None, :, None]
    table = np.stack([(held[:, None, :] // per_chunk) ^ parts, np.broadcast_to((held % per_chunk)[:, None, :], (loop_size, seg_size, loop_size))], axis=-1)
    table = table.reshape(loop_size * seg_size, 2 * loop_size)
    own_genes = np.argmax(held == np.arange(loop_size)[:, None], axis=1)
    table = jnp.asarray(np.concatenate([table, np.repeat(own_genes, seg_size)[:, None]], axis=1), jnp.int32)
    where = lax.dynamic_slice(table, (place * seg_size + part, 0), (1, table.shape[1]))[0]
    rows = loop_size * genes // seg_size
    own, *away = pl.pallas_call(
        functools.partial(pair_kernel, loop_size),
        out_shape=[jax.ShapeDtypeStruct((rows, genes), jnp.float32)] + [jax.ShapeDtypeStruct((rows, genes), jnp.bfloat16)] * (seg_size - 1),
        in_specs=[pl.BlockSpec(memory_space=pltpu.SMEM)] + [vmem] * loop_size,
        out_specs=[vmem] * seg_size,
        scratch_shapes=[pltpu.VMEM((genes, samples), jnp.bfloat16), pltpu.VMEM((seg_size, rows, genes), jnp.float32)],
        compiler_params=pltpu.CompilerParams(vmem_limit_bytes=2 * (loop_size + 1) * genes * samples * 2 + 3 * seg_size * rows * genes * 4),
        name="pair_sums",
    )(where, *blocks)
    total = own
    for j in range(1, seg_size):
        total = total + move(away[j - 1], sizes, lambda l, s: (l, s ^ j)).astype(jnp.float32)
    return total / (samples * seg_size)


def solution(mesh):
    return jax.shard_map(
        shards,
        mesh=mesh,
        in_specs=(P("seg", "loop"), P(None, None, "loop"), P("loop"), P("loop")),
        out_specs=P("seg", "loop"),
        check_vma=False,
    )
```

```python
import functools
import math

import jax
import jax.numpy as jnp
import numpy as np
from jax import lax
from jax.experimental import pallas as pl
from jax.experimental.pallas import tpu as pltpu
from jax.sharding import PartitionSpec as P


AXES = ("loop", "seg")
DOSAGE_MAX, WEIGHT_MAX = 3.0, 0.109375
MASK_ROWS = 16


def ring_next(loop_size, place):
    if place % 2 == 0:
        return place + 2 if place + 2 < loop_size else loop_size - 1
    return place - 2 if place >= 3 else 0


def move(value, sizes, target):
    loop_size, seg_size = sizes
    pairs = []
    for place in range(loop_size):
        for part in range(seg_size):
            to = target(place, part)
            pairs.append((place * seg_size + part, to[0] * seg_size + to[1]))
    return lax.ppermute(value, AXES, pairs)


def stage_kernel(weights_ref, first_ref, last_ref, near_ref, home_ref, tile_ref, window_ref, sems):
    place, part = lax.axis_index("loop"), lax.axis_index("seg")
    n_slots = weights_ref.shape[0]
    half = tile_ref.shape[0]
    far_slot = (place % 2) * (n_slots - 1)
    near_slot = n_slots - 1 - far_slot
    rows = pl.ds(pl.multiple_of((part % 2) * half, half), half)
    copies = [
        pltpu.make_async_copy(first_ref, window_ref.at[0], sems.at[0]),
        pltpu.make_async_copy(last_ref, window_ref.at[1], sems.at[1]),
        pltpu.make_async_copy(weights_ref.at[near_slot, rows], tile_ref, sems.at[2]),
        pltpu.make_async_copy(weights_ref.at[n_slots // 2], home_ref, sems.at[3]),
    ]
    for copy in copies:
        copy.start()
    for copy in copies[:3]:
        copy.wait()
    first, last = window_ref[0], window_ref[1]
    covered = (near_slot >= first) & (near_slot <= last)
    near_ref[:half, :] = jnp.where(covered, tile_ref[...], jnp.zeros((), tile_ref.dtype))
    covered = (far_slot >= first) & (far_slot <= last) & (place > 0) & (place < lax.axis_size("loop") - 1)
    mask = jnp.where(covered, 1.0, 0.0)
    near_ref[half:, :] = jnp.broadcast_to(mask, (MASK_ROWS, mask.shape[1])).astype(near_ref.dtype)
    copies[3].wait()


def pair_kernel(n_blocks, where_ref, *refs):
    blocks, own_ref, away_refs = refs[:n_blocks], refs[n_blocks], refs[n_blocks + 1 : -2]
    column_ref, sums_ref = refs[-2:]
    genes = column_ref.shape[0]
    for k, block in enumerate(blocks):

        @pl.when(where_ref[2 * n_blocks] == k)
        def _():
            column_ref[...] = block[...]

    column = column_ref[...].T
    for k, block in enumerate(blocks):
        product = jnp.dot(block[...], column, preferred_element_type=jnp.float32)
        row = pl.multiple_of(where_ref[2 * k + 1] * genes, genes)
        sums_ref[where_ref[2 * k], pl.ds(row, genes), :] = product
    own_ref[...] = sums_ref[0]
    for j, away_ref in enumerate(away_refs):
        away_ref[...] = sums_ref[j + 1].astype(jnp.bfloat16)


def shards(dosage, weight_tiles, first_tile, last_tile):
    loop_size, seg_size = sizes = (lax.axis_size("loop"), lax.axis_size("seg"))
    place, part = lax.axis_index("loop"), lax.axis_index("seg")
    n_slots, block, genes = weight_tiles.shape
    samples = dosage.shape[0]
    side = part % 2
    half = block // 2

    vmem = pl.BlockSpec(memory_space=pltpu.VMEM)
    hbm = pl.BlockSpec(memory_space=pltpu.HBM)
    tile_of = lambda n: jax.ShapeDtypeStruct((n, genes), weight_tiles.dtype)
    far_half = lax.dynamic_slice(weight_tiles, ((place % 2) * (n_slots - 1), side * half, 0), (1, half, genes))[0]
    near_half, home_tile = pl.pallas_call(
        stage_kernel,
        out_shape=(tile_of(half + MASK_ROWS), tile_of(block)),
        in_specs=[hbm] * 3,
        out_specs=[vmem] * 2,
        scratch_shapes=[pltpu.VMEM((half, genes), weight_tiles.dtype), pltpu.VMEM((2, 1, genes), jnp.int32), pltpu.SemaphoreType.DMA((4,))],
        compiler_params=pltpu.CompilerParams(vmem_limit_bytes=8 * block * genes * 2),
        name="stage",
        cost_estimate=pl.CostEstimate(flops=0, bytes_accessed=4 * block * genes, transcendentals=0),
    )(*[pltpu.with_memory_space_constraint(x, pltpu.HBM) for x in (weight_tiles, first_tile.reshape(1, -1), last_tile.reshape(1, -1))])

    def outward(step):
        def target(l, s):
            to = l + step if l % 2 else l - step
            if 0 <= to < loop_size:
                return to, s
            return (l, s ^ 1) if step == 1 else (l ^ 1, s)

        return target

    partner = lambda l, s: (l ^ 1, s)
    sibling = lambda l, s: (l, s ^ 1)

    scale = 2.0 ** math.floor(math.log2(float(jnp.finfo(jnp.float16).max) / (block * DOSAGE_MAX * WEIGHT_MAX)))

    def packed(term):
        return (term * scale).astype(jnp.float16)

    def product(tile):
        return lax.dot_general(tile, dosage, (((0,), (1,)), ((), ())), preferred_element_type=jnp.float32)

    def term(mine, other):
        lower = jnp.where(side == 0, mine, other)
        upper = jnp.where(side == 0, other, mine)
        return product(jnp.concatenate([lower, upper], axis=0))

    far_half = move(far_half, sizes, outward(1))
    near_half = move(near_half, sizes, partner)
    home_term = product(home_tile)
    far_half, _ = lax.optimization_barrier((far_half, home_term))
    home_term = move(packed(home_term), sizes, partner)
    far_term = term(far_half, move(far_half, sizes, sibling))
    near_half, _ = lax.optimization_barrier((near_half, far_term))
    near_half, far_mask = near_half[:half], near_half[half]
    far_term = move(packed(far_term), sizes, outward(2))
    near_term = term(near_half, move(near_half, sizes, sibling))
    far_term = jnp.where(far_mask[:, None] > 0, far_term.astype(jnp.float32), 0.0)
    ready = lax.optimization_barrier(near_term + home_term.astype(jnp.float32) * (1.0 / scale))
    projection = (ready + far_term * (1.0 / scale)).astype(jnp.bfloat16)

    ahead = [ring_next(loop_size, l) for l in range(loop_size)]
    behind = [ahead.index(l) for l in range(loop_size)]
    blocks, sources = [projection], [list(range(loop_size))]
    forth = back = projection
    forth_from = back_from = sources[0]
    rounds = loop_size // 2 - 1
    for step in range(rounds):
        if step == rounds - 1:
            opposite = jnp.where(side == 0, forth, back)
            opposite = move(opposite, sizes, lambda l, s: (behind[behind[l]] if s % 2 else ahead[ahead[l]], s))
            opposite_from = [forth_from[behind[behind[l]]] for l in range(loop_size)]
        forth = move(forth, sizes, lambda l, s: (ahead[l], s))
        forth_from = [forth_from[behind[l]] for l in range(loop_size)]
        back = move(back, sizes, lambda l, s: (behind[l], s))
        back_from = [back_from[ahead[l]] for l in range(loop_size)]
        blocks += [forth, back]
        sources += [forth_from, back_from]
    blocks.append(opposite)
    sources.append(opposite_from)

    per_chunk = loop_size // seg_size
    held = np.array(sources).T ^ 1
    parts = np.arange(seg_size)[None, :, None]
    table = np.stack([(held[:, None, :] // per_chunk) ^ parts, np.broadcast_to((held % per_chunk)[:, None, :], (loop_size, seg_size, loop_size))], axis=-1)
    table = table.reshape(loop_size * seg_size, 2 * loop_size)
    own_genes = np.argmax(held == np.arange(loop_size)[:, None], axis=1)
    table = jnp.asarray(np.concatenate([table, np.repeat(own_genes, seg_size)[:, None]], axis=1), jnp.int32)
    where = lax.dynamic_slice(table, (place * seg_size + part, 0), (1, table.shape[1]))[0]
    rows = loop_size * genes // seg_size
    own, *away = pl.pallas_call(
        functools.partial(pair_kernel, loop_size),
        out_shape=[jax.ShapeDtypeStruct((rows, genes), jnp.float32)] + [jax.ShapeDtypeStruct((rows, genes), jnp.bfloat16)] * (seg_size - 1),
        in_specs=[pl.BlockSpec(memory_space=pltpu.SMEM)] + [vmem] * loop_size,
        out_specs=[vmem] * seg_size,
        scratch_shapes=[pltpu.VMEM((genes, samples), jnp.bfloat16), pltpu.VMEM((seg_size, rows, genes), jnp.float32)],
        compiler_params=pltpu.CompilerParams(vmem_limit_bytes=2 * (loop_size + 1) * genes * samples * 2 + 3 * seg_size * rows * genes * 4),
        name="pair_sums",
    )(where, *blocks)
    total = own
    for j in range(1, seg_size):
        total = total + move(away[j - 1], sizes, lambda l, s: (l, s ^ j)).astype(jnp.float32)
    return total / (samples * seg_size)


def solution(mesh):
    return jax.shard_map(
        shards,
        mesh=mesh,
        in_specs=(P("seg", "loop"), P(None, None, "loop"), P("loop"), P("loop")),
        out_specs=P("seg", "loop"),
        check_vma=False,
    )
```
